32 devices in a mesh: user: 4 (over x, core), item: 8 (over z, y).
Axes of the slice: x: 2, y: 2, z: 4, core: 2. Of those that a mesh axis runs over, the one named last changes fastest.
Arguments:
- item_feats: bfloat16 [131072, 1024], P(('user', 'item')), may hold values from -30 to 30
- first_weight: bfloat16 [1024, 512], replicated, may hold values from -0.1875 to 0.1875
- second_weight: bfloat16 [512, 256], replicated, may hold values from -0.25 to 0.25
- counts: int32 [131072], P(('user', 'item')), may hold values from 1 to 245760
- user_embed: bfloat16 [8192, 256], P(('user', 'item')), may hold values from -1 to 1
- list_owner: int32 [4096, 1], P(('user', 'item')), may hold values from 0 to 31, as said below
- list_slot: int32 [4096], P(('user', 'item')), may hold values from 0 to 31
- positive: int32 [8192], P(('user', 'item')), may hold values from 0 to 2047
Outputs:
- user_loss: float32 [8192], P(('user', 'item'))
- user_gradient: float32 [8192, 256], P(('user', 'item'))
- first_gradient: float32 [1024, 512], replicated
- second_gradient: float32 [512, 256], replicated
The draws below stay inside these ranges and needn't reach their ends.
Inputs may be any that keep to these rules, and one draw needn't show every extreme that they name: `list_owner`: the rows of one device (128 of them, an aligned block) name any one owner at most 8 times; in every draw one owner is named exactly 8 times in the rows of every device.
All inputs are finite; a program needn't handle non-finite values.
Results may differ from the reference program's by a relative error of at most 0.0064.
Values may be sent and summed in bfloat16 or wider, within the bound.
No kernel may reach another device: no remote copies, remote signals or barrier semaphores. Data moves between devices by JAX's collectives and lax.ppermute only.
A program may use at most 192 MiB of HBM per device.

```python
import math
import jax
import jax.numpy as jnp
from jax import lax

FEAT = 1024
HID = 512
EMB = 256
BLK = 128
NQ = 8
QB = 16
IBLK_DEV = 32
OWNERS = 32
REQ = 128
CAP = 8
USERS = 8192
ITEMS = 131072
NBLK = 1024
UG = 32
CAND = 2048


def draw_item_feats(key, part):
    first_key, second_key = jax.random.split(key, 2)
    scales = jnp.exp(jax.random.uniform(first_key, (ITEMS, 1), minval=math.log(0.5), maxval=math.log(5.0)))
    values = scales * jax.random.truncated_normal(second_key, -6.0, 6.0, (ITEMS, FEAT))
    return values.astype(jnp.bfloat16)


def draw_user_embed(key, part):
    first_key, second_key = jax.random.split(key, 2)
    scales = jnp.exp(jax.random.uniform(first_key, (USERS, 1), minval=math.log(1.0 / 64.0), maxval=math.log(10.0 / 64.0)))
    values = scales * jax.random.truncated_normal(second_key, -6.0, 6.0, (USERS, EMB))
    return values.astype(jnp.bfloat16)


def draw_counts(key, part):
    first_key, second_key = jax.random.split(key)
    mantissa = jax.random.randint(first_key, (ITEMS,), 1, 16)
    exponent = jax.random.randint(second_key, (ITEMS,), 0, 15)
    return (mantissa * jnp.left_shift(jnp.ones_like(exponent), exponent)).astype(jnp.int32)


def draw_list_owner(key, part):
    rows_each = NQ * QB
    hottest = jax.random.randint(jax.random.fold_in(key, 11), (), 0, OWNERS)
    base = (jnp.arange(OWNERS * CAP, dtype=jnp.int32) // CAP).astype(jnp.int32)

    def one_device(device_key):
        first_key, second_key = jax.random.split(device_key)
        shuffled = jax.random.permutation(first_key, base)
        order = jnp.argsort((shuffled == hottest).astype(jnp.int32), stable=True)
        others = shuffled[order][:rows_each - CAP]
        chosen = jnp.concatenate([jnp.full((CAP,), hottest, jnp.int32), others])
        return jax.random.permutation(second_key, chosen)
    device_keys = jax.random.split(jax.random.fold_in(key, 12), OWNERS)
    return jax.vmap(one_device)(device_keys).reshape(OWNERS * rows_each, 1).astype(jnp.int32)


def set_ends(result, own_key, low, largest):
    dims = result.shape
    place = [jax.random.randint(jax.random.fold_in(own_key, axis), (), 0, dims[axis]) for axis in range(len(dims))]
    result = result.at[tuple(place)].set(low)
    longest = dims.index(max(dims))
    place[longest] = (place[longest] + 1) % dims[longest]
    return result.at[tuple(place)].set(largest)


def normal_values(key, dims, spread, limit, held_as=jnp.bfloat16):
    return jnp.clip(spread * jax.random.normal(key, dims, jnp.float32), -limit, limit).astype(held_as)


def setup_inputs(seed: int = 0) -> dict:
    key_list = jax.random.split(jax.random.key(seed), 9)
    return {
        "item_feats": draw_item_feats(jax.random.fold_in(key_list[8], 71), 0),
        "first_weight": normal_values(key_list[1], (FEAT, HID), FEAT ** -0.5, 0.1875),
        "second_weight": normal_values(key_list[2], (HID, EMB), HID ** -0.5, 0.25),
        "counts": draw_counts(jax.random.fold_in(key_list[8], 71), 0),
        "user_embed": draw_user_embed(jax.random.fold_in(key_list[8], 71), 0),
        "list_owner": draw_list_owner(jax.random.fold_in(key_list[8], 71), 0),
        "list_slot": set_ends(jax.random.randint(key_list[6], (OWNERS * REQ,), 0, IBLK_DEV), jax.random.fold_in(key_list[6], 1), 0, IBLK_DEV - 1).astype(jnp.int32),
        "positive": set_ends(jax.random.randint(key_list[7], (USERS,), 0, CAND), jax.random.fold_in(key_list[7], 1), 0, CAND - 1).astype(jnp.int32),
    }


LOGIT_SCALE = 20.0
LOSS_SCALE = 4096.0
NORM_EPSILON = 1e-06

def tower_forward(feats_rows, first_weight, second_weight):
    linear_one = jnp.dot(feats_rows, first_weight, preferred_element_type=jnp.float32)
    hidden = jnp.maximum(linear_one, 0.0).astype(jnp.bfloat16)
    tower_out = jnp.dot(hidden, second_weight, preferred_element_type=jnp.float32)
    item_norm = lax.rsqrt(lax.optimization_barrier(jnp.sum(tower_out * tower_out, axis=1, keepdims=True)) + NORM_EPSILON)
    return (hidden, tower_out, item_norm)

def reference(item_feats, first_weight, second_weight, counts, user_embed, list_owner, list_slot, positive):
    shard_rows = IBLK_DEV * BLK
    feats_shards = item_feats.reshape(OWNERS, shard_rows, FEAT)

    def forward(feats_rows):
        hidden, tower_out, item_norm = tower_forward(feats_rows, first_weight, second_weight)
        return (hidden, (tower_out * item_norm).astype(jnp.bfloat16))
    hidden_all, item_vector = lax.map(forward, feats_shards)
    item_vector = item_vector.reshape(NBLK, BLK, EMB)
    log_count = jnp.log(counts.astype(jnp.float32)).astype(jnp.bfloat16).reshape(NBLK, BLK)
    user_float = user_embed.astype(jnp.float32)
    user_norm = lax.rsqrt(lax.optimization_barrier(jnp.sum(user_float * user_float, axis=1, keepdims=True)) + NORM_EPSILON)
    user_vector = (user_float * user_norm).astype(jnp.bfloat16)
    block_ids = (list_owner[:, 0] * IBLK_DEV + list_slot).astype(jnp.int32).reshape(OWNERS, NQ, QB)
    group_users = user_vector.reshape(OWNERS, NQ, UG, EMB)
    group_pos = positive.reshape(OWNERS, NQ, UG)
    labels = jnp.arange(CAND, dtype=jnp.int32)

    def per_device(gradient_sum, inputs):
        blocks, members, targets = inputs
        candidates = item_vector[blocks].reshape(NQ, CAND, EMB).astype(jnp.float32)
        cand_logs = log_count[blocks].reshape(NQ, CAND).astype(jnp.float32)
        members_float = members.astype(jnp.float32)
        scores = LOGIT_SCALE * jnp.einsum('gue,gce->guc', members_float, candidates) - cand_logs[:, None, :]
        exp_scores = jnp.exp(scores)
        totals = lax.optimization_barrier(jnp.sum(exp_scores, axis=2))
        is_positive = labels[None, None, :] == targets[:, :, None]
        losses = jnp.log(totals) - lax.optimization_barrier(jnp.sum(jnp.where(is_positive, scores, 0.0), axis=2))
        score_grad = (LOSS_SCALE / USERS * (exp_scores / totals[:, :, None] - is_positive.astype(jnp.float32))).astype(jnp.bfloat16)
        grad_float = score_grad.astype(jnp.float32)
        vector_grad = LOGIT_SCALE * jnp.einsum('guc,gce->gue', grad_float, candidates)
        cand_grad = (LOGIT_SCALE * jnp.einsum('guc,gue->gce', grad_float, members_float)).astype(jnp.bfloat16)
        gradient_sum = gradient_sum.at[blocks.reshape(REQ)].add(cand_grad.reshape(REQ, BLK, EMB).astype(jnp.float32))
        return (gradient_sum, (losses, vector_grad))
    start_sum = jnp.zeros((NBLK, BLK, EMB), jnp.float32)
    item_gradient, (losses, vector_grad) = lax.scan(per_device, start_sum, (block_ids, group_users, group_pos))
    user_loss = losses.reshape(USERS)
    vector_grad = vector_grad.reshape(USERS, EMB)
    user_projection = lax.optimization_barrier(jnp.sum(user_float * vector_grad, axis=1, keepdims=True))
    user_gradient = vector_grad * user_norm - user_float * (user_projection * user_norm * user_norm * user_norm)
    grad_shards = item_gradient.reshape(OWNERS, shard_rows, EMB)

    def backward(totals_pair, inputs):
        feats_rows, hidden, gradient_rows = inputs
        tower_out = jnp.dot(hidden, second_weight, preferred_element_type=jnp.float32)
        item_norm = lax.rsqrt(lax.optimization_barrier(jnp.sum(tower_out * tower_out, axis=1, keepdims=True)) + NORM_EPSILON)
        projection = lax.optimization_barrier(jnp.sum(tower_out * gradient_rows, axis=1, keepdims=True))
        out_gradient = (gradient_rows * item_norm - tower_out * (projection * item_norm * item_norm * item_norm)).astype(jnp.bfloat16)
        second_total = totals_pair[1] + jnp.dot(hidden.T, out_gradient, preferred_element_type=jnp.float32)
        act_gradient = jnp.where(hidden > 0, jnp.dot(out_gradient, second_weight.T, preferred_element_type=jnp.float32), 0.0).astype(jnp.bfloat16)
        first_total = totals_pair[0] + jnp.dot(feats_rows.T, act_gradient, preferred_element_type=jnp.float32)
        return ((first_total, second_total), None)
    zeros_pair = (jnp.zeros((FEAT, HID), jnp.float32), jnp.zeros((HID, EMB), jnp.float32))
    (first_gradient, second_gradient), unused = lax.scan(backward, zeros_pair, (feats_shards, hidden_all, grad_shards))
    return (user_loss, user_gradient, first_gradient, second_gradient)
```

```python
import functools

import jax
import jax.numpy as jnp
import numpy as np
from jax import lax
from jax.experimental import pallas as pl
from jax.experimental.pallas import tpu as pltpu
from jax.sharding import PartitionSpec as P

BLK = 128
NQ = 8
QB = 16
SUB = 4

LOGIT_SCALE = 20.0
LOSS_SCALE = 4096.0
NORM_EPSILON = 1e-06

AXES = ("user", "item")
F32 = jnp.float32
BF16 = jnp.bfloat16
I32 = jnp.int32


class Links:
    def __init__(self):
        users = lax.axis_size("user")
        items = lax.axis_size("item")
        self.devices = users * items
        item_bits = items.bit_length() - 1
        user_bits = users.bit_length() - 1
        self.y = list(range(item_bits - 2))
        self.z = [item_bits - 1, item_bits - 2]
        self.core = item_bits
        self.x = list(range(item_bits + 1, item_bits + user_bits))

    def swap(self, value, mask):
        pairs = [(d, d ^ mask) for d in range(self.devices)]
        return lax.ppermute(value, AXES, pairs)


def join(parts):
    return parts[0] if len(parts) == 1 else jnp.concatenate(parts, axis=0)


def gather_plan(links):
    masks = [[0]]
    steps = []

    def add(bit, sources):
        steps.append((1 << bit, list(sources)))
        masks.append([m ^ (1 << bit) for s in sources for m in masks[s]])
        return len(masks) - 1

    base = [0]
    for bit in links.z:
        base.append(add(bit, base))
    first, second = base[:-1], base[-1:]
    for bit_a, bit_b in zip(links.y + links.x, links.x + links.y):
        new_a = add(bit_a, first)
        new_b = add(bit_b, second)
        first, second = first + [new_a], second + [new_b]
    return masks, steps


def scalar_copy(pieces, scratch, sems, per):
    offset = 0
    copies = []
    for index, piece in enumerate(pieces):
        rows = piece.shape[0]
        copies.append(
            pltpu.make_async_copy(piece, scratch.at[pl.ds(offset, rows), :], sems.at[index])
        )
        offset += rows
    return copies


def score_kernel(n_pieces, group, ul, tl, vq, cblk, nch, *refs):
    pieces = refs[:n_pieces]
    vectors, logs, loc, exp_out, totals_out, pos_out, users, t_acc, p_acc, sems = refs[n_pieces:]
    copies = scalar_copy(pieces, users, sems, group)
    for copy in copies:
        copy.start()
    t_acc[...] = jnp.zeros_like(t_acc)
    p_acc[...] = jnp.zeros_like(p_acc)
    for copy in copies:
        copy.wait()
    rows_iota = lax.broadcasted_iota(I32, (BLK, BLK), 0)
    lane_group = lax.broadcasted_iota(I32, (1, BLK), 1) // group

    def step(c, carry):
        first = pl.multiple_of(cblk[c] * BLK, BLK)
        block = vectors[pl.ds(first, BLK), :]
        members = jnp.concatenate(
            [users[pl.ds(pl.multiple_of(ul[c * SUB + i] * group, group), group), :] for i in range(SUB)],
            axis=0,
        )
        dots = lax.dot_general(block, members, (((1,), (1,)), ((), ())), preferred_element_type=F32)
        scores = LOGIT_SCALE * dots - logs[pl.ds(first, BLK), :]
        exp_scores = jnp.exp(scores)
        exp_out[pl.ds(pl.multiple_of(c * BLK, BLK), BLK), :] = exp_scores
        total = jnp.sum(exp_scores, axis=0, keepdims=True)
        is_positive = rows_iota == loc[pl.ds(c, 1), :]
        chosen = jnp.sum(jnp.where(is_positive, scores, 0.0), axis=0, keepdims=True)
        for i in range(SUB):
            keep = jnp.logical_and(lane_group == i, vq[c * SUB + i] > 0)
            row = tl[c * SUB + i]
            t_acc[pl.ds(row, 1), :] += jnp.where(keep, total, 0.0)
            p_acc[pl.ds(row, 1), :] += jnp.where(keep, chosen, 0.0)
        return carry

    lax.fori_loop(0, nch[0], step, 0)
    packed_rows = totals_out.shape[0]
    for acc, out in ((t_acc, totals_out), (p_acc, pos_out)):
        value = acc[...]
        both = value + pltpu.roll(value, 2 * group, axis=1)
        acc[...] = both + pltpu.roll(both, group, axis=1)
        packed = jnp.zeros((packed_rows, BLK), F32)
        for i in range(SUB):
            packed += jnp.where(lane_group == i, acc[pl.ds(i, packed_rows, stride=SUB), :], 0.0)
        out[...] = packed


def grad_kernel(
    n_pieces, group, scale, columns, with_items, ul, tl, vq, cblk, nch, *refs
):
    pieces = refs[:n_pieces]
    rest = refs[n_pieces:]
    vectors, exp_in, loc, totals = rest[:4]
    if with_items:
        keep_out, send_out, item_out, users, t_rep, v_acc, sems = rest[4:]
    else:
        keep_out, send_out, users, t_rep, v_acc, sems = rest[4:]
    copies = scalar_copy(pieces, users, sems, group)
    for copy in copies:
        copy.start()
    v_acc[...] = jnp.zeros_like(v_acc)
    if with_items:
        item_out[...] = jnp.zeros_like(item_out)
    rows_iota = lax.broadcasted_iota(I32, (BLK, BLK), 0)
    lane_group = lax.broadcasted_iota(I32, (1, BLK), 1) // group
    inverse = scale / totals[...]
    packed_rows = totals.shape[0]
    for i in range(SUB):
        part = jnp.where(lane_group == i, inverse, 0.0)
        part = part + pltpu.roll(part, 2 * group, axis=1)
        t_rep[pl.ds(i, packed_rows, stride=SUB), :] = part + pltpu.roll(part, group, axis=1)
    for copy in copies:
        copy.wait()
    low, high = columns

    def step(c, carry):
        first = pl.multiple_of(cblk[c] * BLK, BLK)
        weight = jnp.zeros((1, BLK), F32)
        for i in range(SUB):
            keep = jnp.logical_and(lane_group == i, vq[c * SUB + i] > 0)
            weight += jnp.where(keep, t_rep[pl.ds(tl[c * SUB + i], 1), :], 0.0)
        is_positive = rows_iota == loc[pl.ds(c, 1), :]
        exp_scores = exp_in[pl.ds(pl.multiple_of(c * BLK, BLK), BLK), :]
        grad = (exp_scores * weight - jnp.where(is_positive, scale, 0.0)).astype(BF16)
        starts = [pl.multiple_of(ul[c * SUB + i] * group, group) for i in range(SUB)]
        if with_items:
            members = jnp.concatenate([users[pl.ds(s, group), :] for s in starts], axis=0)
            item_out[pl.ds(first, BLK), :] += jnp.dot(grad, members, preferred_element_type=F32)
        block = vectors[pl.ds(first, BLK), low:high]
        parts = lax.dot_general(grad, block, (((0,), (0,)), ((), ())), preferred_element_type=F32)
        for i in range(SUB):
            v_acc[pl.ds(starts[i], group), :] += parts[i * group : (i + 1) * group]
        return carry

    lax.fori_loop(0, nch[0], step, 0)
    half = v_acc.shape[0] // 2
    keep_out[...] = (LOGIT_SCALE * v_acc[pl.ds(0, half), :]).astype(keep_out.dtype)
    send_out[...] = (LOGIT_SCALE * v_acc[pl.ds(half, half), :]).astype(BF16)


def any_spec():
    return pl.BlockSpec(memory_space=pl.ANY)


def vmem_spec():
    return pl.BlockSpec(memory_space=pltpu.VMEM)


def body(
    item_feats, first_weight, second_weight, counts, user_embed, list_owner, list_slot, positive
):
    links = Links()
    devices = links.devices
    me = lax.axis_index(AXES)
    item_rows, _ = item_feats.shape
    own_blocks = item_rows // BLK
    user_rows, emb = user_embed.shape
    requests = list_slot.shape[0]
    capacity = 2 * requests // devices
    group = user_rows // NQ
    all_users = user_rows * devices
    slots = devices * capacity
    lists = devices * NQ
    core = 1 << links.core

    user_float = user_embed.astype(F32)
    user_norm = lax.rsqrt(jnp.sum(user_float * user_float, axis=1, keepdims=True) + NORM_EPSILON)
    user_vector = (user_float * user_norm).astype(BF16)

    masks, steps = gather_plan(links)
    order = [m for piece in masks for m in piece]
    order = order + [m ^ core for m in order]
    place = np.zeros((devices,), np.int32)
    place[np.array(order)] = np.arange(devices, dtype=np.int32)

    pieces = [user_vector]
    for mask, sources in steps:
        pieces.append(links.swap(join([pieces[s] for s in sources]), mask))
    other = [links.swap(piece, core) for piece in pieces]
    all_pieces = pieces + other

    owners = list_owner[:, 0]
    same_owner = owners[:, None] == owners[None, :]
    request = jnp.arange(requests, dtype=I32)
    rank = jnp.sum((same_owner & (request[None, :] < request[:, None])).astype(I32), axis=1)
    position = owners * capacity + rank
    hit = position[:, None] == jnp.arange(slots, dtype=I32)[None, :]
    request_code = jnp.sum(jnp.where(hit, request[:, None] + 1, 0), axis=0)
    slot_code = jnp.sum(jnp.where(hit, list_slot[:, None], 0), axis=0)
    tables = jnp.concatenate([request_code, slot_code, positive])
    pad = -tables.shape[0] % (8 * BLK)
    tables = jnp.pad(tables, (0, pad)).reshape(1, -1, BLK)
    t_masks = [0]
    for bit in links.z + links.y + links.x + [links.core]:
        tables = jnp.concatenate([tables, links.swap(tables, 1 << bit)], axis=0)
        t_masks = t_masks + [m ^ (1 << bit) for m in t_masks]
    tables = tables.reshape(devices, -1)
    t_masks = np.array(t_masks)
    codes = lax.dynamic_slice(tables, (0, me * capacity), (devices, capacity)).reshape(-1)
    blocks = lax.dynamic_slice(tables, (0, slots + me * capacity), (devices, capacity)).reshape(-1)
    positions = tables[:, 2 * slots : 2 * slots + user_rows].reshape(lists, group)

    valid = codes > 0
    req = jnp.maximum(codes - 1, 0)
    in_list = req // QB
    kth = req % QB
    place_of = jnp.asarray(np.repeat(place[t_masks], capacity), I32)
    mask_of = jnp.asarray(np.repeat(t_masks, capacity), I32)
    source_of = jnp.asarray(np.repeat(np.arange(devices), capacity), I32)
    slot_index = jnp.arange(slots, dtype=I32)
    same_block = (blocks[:, None] == blocks[None, :]) & valid[None, :]
    block_rank = jnp.sum((same_block & (slot_index[None, :] < slot_index[:, None])).astype(I32), axis=1)
    block_index = jnp.arange(own_blocks, dtype=I32)
    one_hot = ((blocks[:, None] == block_index[None, :]) & valid[:, None]).astype(I32)
    chunks_of = (jnp.sum(one_hot, axis=0) + SUB - 1) // SUB
    start_of = jnp.sum(
        jnp.where(block_index[None, :] < block_index[:, None], chunks_of[None, :], 0), axis=1
    )
    n_chunks = jnp.sum(chunks_of).reshape(1)
    max_chunks = (slots + (SUB - 1) * own_blocks) // SUB
    spots = max_chunks * SUB
    spot_of = jnp.sum(one_hot * start_of[None, :], axis=1) * SUB + block_rank
    spot_of = jnp.where(valid, spot_of, -1)
    at_spot = spot_of[None, :] == jnp.arange(spots, dtype=I32)[:, None]

    def to_spot(value):
        return jnp.sum(jnp.where(at_spot, value[None, :], 0), axis=1)

    ul = to_spot(place_of * NQ + in_list)
    tl = to_spot((me ^ mask_of) * NQ + in_list)
    vq = to_spot(jnp.ones_like(codes))
    kq = to_spot(kth)
    jl = to_spot(source_of * NQ + in_list)
    chunk_index = jnp.arange(max_chunks, dtype=I32)
    cblk = (
        jnp.sum((start_of[None, :] <= chunk_index[:, None]).astype(I32), axis=1) - 1
    )
    local = positions[jl] - kq[:, None] * BLK
    local = jnp.where((local >= 0) & (local < BLK) & (vq[:, None] > 0), local, -1)
    local = local.reshape(max_chunks, SUB * group)

    linear_one = jnp.dot(item_feats, first_weight, preferred_element_type=F32)
    hidden = jnp.maximum(linear_one, 0.0).astype(BF16)
    tower_out = jnp.dot(hidden, second_weight, preferred_element_type=F32)
    item_norm = lax.rsqrt(jnp.sum(tower_out * tower_out, axis=1, keepdims=True) + NORM_EPSILON)
    vectors = (tower_out * item_norm).astype(BF16)
    logs = jnp.log(counts.astype(F32)).astype(BF16).astype(F32)
    logs = jnp.broadcast_to(logs[:, None], (item_rows, BLK))

    n_pieces = len(all_pieces)
    packed_rows = all_users // BLK
    limit = pltpu.CompilerParams(vmem_limit_bytes=60 * 1024 * 1024)
    exp_scores, part_totals, part_pos = pl.pallas_call(
        functools.partial(score_kernel, n_pieces, group),
        out_shape=(
            jax.ShapeDtypeStruct((max_chunks * BLK, BLK), F32),
            jax.ShapeDtypeStruct((packed_rows, BLK), F32),
            jax.ShapeDtypeStruct((packed_rows, BLK), F32),
        ),
        grid_spec=pltpu.PrefetchScalarGridSpec(
            num_scalar_prefetch=5,
            grid=(1,),
            in_specs=[any_spec()] * n_pieces + [vmem_spec()] * 3,
            out_specs=[vmem_spec()] * 3,
            scratch_shapes=[
                pltpu.VMEM((all_users, emb), BF16),
                pltpu.VMEM((lists, BLK), F32),
                pltpu.VMEM((lists, BLK), F32),
                pltpu.SemaphoreType.DMA((n_pieces,)),
            ],
        ),
        compiler_params=limit,
        name="scores",
    )(ul, tl, vq, cblk, n_chunks, *all_pieces, vectors, logs, local)

    sums = jnp.concatenate([part_totals, part_pos], axis=0)
    for bit in [links.core] + links.x + links.y + links.z[::-1]:
        sums = sums + links.swap(sums, 1 << bit)
    totals = sums[:packed_rows]
    own_rows = user_rows // BLK
    own_totals = lax.dynamic_slice(sums, (me * own_rows, 0), (own_rows, BLK))
    own_pos = lax.dynamic_slice(sums, (packed_rows + me * own_rows, 0), (own_rows, BLK))
    user_loss = (jnp.log(own_totals) - own_pos).reshape(user_rows)

    keep_type = F32 if all_users <= 8192 else BF16
    width = emb if all_users <= 8192 else BLK
    half_users = all_users // 2
    keeps, sends = [], []
    for low in range(0, emb, width):
        with_items = low == 0
        shapes = [
            jax.ShapeDtypeStruct((half_users, width), keep_type),
            jax.ShapeDtypeStruct((half_users, width), BF16),
        ]
        if with_items:
            shapes.append(jax.ShapeDtypeStruct((item_rows, emb), F32))
        outs = pl.pallas_call(
            functools.partial(
                grad_kernel, n_pieces, group, LOSS_SCALE / all_users, (low, low + width), with_items
            ),
            out_shape=shapes,
            grid_spec=pltpu.PrefetchScalarGridSpec(
                num_scalar_prefetch=5,
                grid=(1,),
                in_specs=[any_spec()] * n_pieces + [vmem_spec()] * 4,
                out_specs=[vmem_spec()] * len(shapes),
                scratch_shapes=[
                    pltpu.VMEM((all_users, emb), BF16),
                    pltpu.VMEM((lists, BLK), F32),
                    pltpu.VMEM((all_users, width), F32),
                    pltpu.SemaphoreType.DMA((n_pieces,)),
                ],
            ),
            compiler_params=limit,
            name="grads",
        )(ul, tl, vq, cblk, n_chunks, *all_pieces, vectors, exp_scores, local, totals)
        keeps.append(outs[0])
        sends.append(outs[1])
        if with_items:
            item_sum = outs[2]
    keep = keeps[0] if len(keeps) == 1 else jnp.concatenate(keeps, axis=1)
    send = sends[0] if len(sends) == 1 else jnp.concatenate(sends, axis=1)

    parts = keep.astype(F32) + links.swap(send, core).astype(F32)
    partial, offset = [], 0
    for piece in masks:
        rows = len(piece) * user_rows
        partial.append(parts[offset : offset + rows])
        offset += rows
    for index in range(len(steps) - 1, -1, -1):
        mask, sources = steps[index]
        arrived = links.swap(partial[index + 1].astype(BF16), mask).astype(F32)
        offset = 0
        for s in sources:
            rows = partial[s].shape[0]
            partial[s] = partial[s] + arrived[offset : offset + rows]
            offset += rows
    vector_grad = partial[0]
    user_projection = jnp.sum(user_float * vector_grad, axis=1, keepdims=True)
    user_gradient = vector_grad * user_norm - user_float * (
        user_projection * user_norm * user_norm * user_norm
    )

    item_gradient = LOGIT_SCALE * item_sum
    projection = jnp.sum(tower_out * item_gradient, axis=1, keepdims=True)
    out_gradient = (
        item_gradient * item_norm - tower_out * (projection * item_norm * item_norm * item_norm)
    ).astype(BF16)
    second_gradient = jnp.dot(hidden.T, out_gradient, preferred_element_type=F32)
    act_gradient = jnp.where(
        hidden > 0, jnp.dot(out_gradient, second_weight.T, preferred_element_type=F32), 0.0
    ).astype(BF16)
    first_gradient = jnp.dot(item_feats.T, act_gradient, preferred_element_type=F32)

    feat, hid = first_weight.shape
    fold = hid // emb
    tall = hid // fold
    packed = jnp.concatenate(
        [first_gradient]
        + [jnp.concatenate([second_gradient[i * tall : (i + 1) * tall] for i in range(fold)], axis=1)],
        axis=0,
    )
    total = sum_all(links, me, packed)
    first_total = total[:feat].astype(F32)
    second_total = jnp.concatenate(
        [total[feat:, i * emb : (i + 1) * emb] for i in range(fold)], axis=0
    ).astype(F32)
    return (user_loss, user_gradient, first_total, second_total)


def sum_all(links, me, value):
    rows = value.shape[0]
    half = rows // 2
    core_bit = (me >> links.core) & 1
    send = lax.dynamic_slice_in_dim(value, (1 - core_bit) * half, half, 0).astype(BF16)
    mine = lax.dynamic_slice_in_dim(value, core_bit * half, half, 0)
    mine = mine + links.swap(send, 1 << links.core).astype(F32)
    plane = links.x + links.y
    ways = 1 << len(plane)
    part = half // ways
    own = sum(((me >> bit) & 1) << i for i, bit in enumerate(plane))

    def mask_of(way):
        return sum(1 << bit for i, bit in enumerate(plane) if (way >> i) & 1)

    arrived = []
    for way in range(1, ways):
        out = lax.dynamic_slice_in_dim(mine, (own ^ way) * part, part, 0).astype(BF16)
        arrived.append(links.swap(out, mask_of(way)))
    own_sum = lax.dynamic_slice_in_dim(mine, own * part, part, 0)
    for item in arrived:
        own_sum = own_sum + item.astype(F32)
    for bit in links.z[::-1]:
        rounded = own_sum.astype(BF16)
        own_sum = rounded.astype(F32) + links.swap(rounded, 1 << bit).astype(F32)
    final = own_sum.astype(BF16)
    quarters = [final] + [links.swap(final, mask_of(way)) for way in range(1, ways)]
    for i in range(len(plane)):
        bit = (own >> i) & 1
        step = 1 << i
        quarters = [jnp.where(bit == 1, quarters[q ^ step], quarters[q]) for q in range(ways)]
    near = jnp.concatenate(quarters, axis=0)
    far = links.swap(near, 1 << links.core)
    return jnp.concatenate(
        [jnp.where(core_bit == 0, near, far), jnp.where(core_bit == 0, far, near)], axis=0
    )


def solution(mesh):
    return jax.shard_map(
        body,
        mesh=mesh,
        in_specs=(
            P(("user", "item"), None),
            P(),
            P(),
            P(("user", "item")),
            P(("user", "item"), None),
            P(("user", "item"), None),
            P(("user", "item")),
            P(("user", "item")),
        ),
        out_specs=(P(("user", "item")), P(("user", "item"), None), P(), P()),
        check_vma=False,
    )
```

```python
import functools

import jax
import jax.numpy as jnp
import numpy as np
from jax import lax
from jax.experimental import pallas as pl
from jax.experimental.pallas import tpu as pltpu
from jax.sharding import PartitionSpec as P

BLK = 128
NQ = 8
QB = 16
SUB = 4
UNROLL = 4
TILE = 512
HEAD = 16

LOGIT_SCALE = 20.0
LOSS_SCALE = 4096.0
NORM_EPSILON = 1e-06

AXES = ("user", "item")
F32 = jnp.float32
BF16 = jnp.bfloat16
I32 = jnp.int32


class Links:
    def __init__(self):
        users = lax.axis_size("user")
        items = lax.axis_size("item")
        self.devices = users * items
        item_bits = items.bit_length() - 1
        user_bits = users.bit_length() - 1
        self.y = list(range(item_bits - 2))
        self.z = [item_bits - 1, item_bits - 2]
        self.core = item_bits
        self.x = list(range(item_bits + 1, item_bits + user_bits))

    def swap(self, value, mask):
        pairs = [(d, d ^ mask) for d in range(self.devices)]
        return lax.ppermute(value, AXES, pairs)


def join(parts):
    return parts[0] if len(parts) == 1 else jnp.concatenate(parts, axis=0)


def gather_plan(links):
    masks = [[0]]
    steps = []

    def add(bit, sources):
        steps.append((1 << bit, list(sources)))
        masks.append([m ^ (1 << bit) for s in sources for m in masks[s]])
        return len(masks) - 1

    base = [0]
    for bit in links.z:
        base.append(add(bit, base))
    first, second = base[:-1], base[-1:]
    for bit_a, bit_b in zip(links.y + links.x, links.x + links.y):
        new_a = add(bit_a, first)
        new_b = add(bit_b, second)
        first, second = first + [new_a], second + [new_b]
    return masks, steps


def piece_copies(pieces, scratch, sems, start, rows, count):
    copies = []
    for piece in pieces:
        for first in range(0, piece.shape[0], count):
            place = len(copies)
            copies.append(
                pltpu.make_async_copy(
                    piece.at[pl.ds(first + start, rows), :],
                    scratch.at[pl.ds(place * rows, rows), :],
                    sems.at[place],
                )
            )
    return copies


def tower_kernel(feats, first_t, second_t, hidden_t, tower, vectors):
    linear = lax.dot_general(
        first_t[...], feats[...], (((1,), (1,)), ((), ())), preferred_element_type=F32
    )
    hidden = jnp.maximum(linear, 0.0).astype(BF16)
    hidden_t[...] = hidden
    out = jnp.dot(second_t[...], hidden, preferred_element_type=F32).T
    tower[...] = out
    norm = lax.rsqrt(jnp.sum(out * out, axis=1, keepdims=True) + NORM_EPSILON)
    vectors[...] = (out * norm).astype(BF16)


class Plan:
    def __init__(self, ref, spots, tiles):
        self.ref = ref
        self.spots = spots
        self.tiles = tiles
        self.chunk_base = 2 * spots
        self.tile_base = self.chunk_base + spots // SUB
        self.size = self.tile_base + tiles + 2

    def ul(self, q):
        return self.ref[q] & 0xFFFF

    def tl(self, q):
        return self.ref[q] >> 16

    def kq(self, q):
        return self.ref[self.spots + q] & 0xFFFF

    def vq(self, q):
        return self.ref[self.spots + q] >> 16

    def cblk(self, c):
        return self.ref[self.chunk_base + c]

    def starts(self, t):
        return self.ref[self.tile_base + t]

    def nch(self):
        return self.ref[self.tile_base + self.tiles]


def plan_kernel(n_pieces, capacity, tile_blocks, sizes, where, masks, *refs):
    pieces = refs[:n_pieces]
    out, positions, raw, wide_a, wide_b, picked, table, count, cursor, sems = refs[n_pieces:]
    layout = Plan(out, *sizes)
    spots = layout.spots
    blocks = count.shape[0] - 1
    devices = picked.shape[0] // 2
    lane, me, half = where[0], where[1], where[2]
    per = raw.shape[0] // devices
    width = raw.shape[1]
    copies = piece_copies(pieces, raw, sems, width, per, width + per)
    for copy in copies:
        copy.start()

    def clear(b, carry):
        count[b] = 0
        return carry

    lax.fori_loop(0, blocks + 1, clear, 0)
    for copy in copies:
        copy.wait()
    wide_a[...] = raw[:, :BLK].astype(F32)
    wide_b[...] = raw[:, BLK:].astype(F32)
    for field in range(2):
        rows = pl.ds(field, devices, stride=per)
        side = jnp.where(half > 0, wide_b[rows, :], wide_a[rows, :])
        picked[pl.ds(field * devices, devices), :] = side.astype(I32)
    move = pltpu.make_async_copy(picked, table, sems.at[0])
    move.start()
    for i, wide in enumerate((wide_a, wide_b)):
        high = wide[pl.ds(2, devices, stride=per), :]
        low = wide[pl.ds(3, devices, stride=per), :]
        positions[pl.ds(i, devices, stride=2), :] = (high * BLK + low).astype(I32)
    move.wait()

    def tally(j, carry):
        for k in range(capacity):
            valid = table[j, lane + k] > 0
            b = jnp.where(valid, table[devices + j, lane + k], blocks)
            count[b] += 1
        return carry

    lax.fori_loop(0, devices, tally, 0)

    def blank(q):
        out[q] = 0
        out[spots + q] = 0

    def place(b, start):
        n = count[b]
        chunks = (n + SUB - 1) // SUB
        cursor[b] = start * SUB

        def name(c, carry):
            out[layout.chunk_base + c] = b
            for i in range(SUB):
                blank(c * SUB + i)
            return carry

        lax.fori_loop(start, start + chunks, name, 0)

        @pl.when(b % tile_blocks == 0)
        def _():
            out[layout.tile_base + b // tile_blocks] = start

        return start + chunks

    total = lax.fori_loop(0, blocks, place, 0)
    out[layout.tile_base + layout.tiles] = total
    for extra in range(UNROLL):
        out[layout.chunk_base + total + extra] = 0
        for i in range(SUB):
            blank((total + extra) * SUB + i)

    def settle(j, carry):
        device = masks[j] ^ me
        fixed = j * NQ + device * (NQ << 16)
        for k in range(capacity):
            code = table[j, lane + k]
            valid = code > 0
            b = jnp.where(valid, table[devices + j, lane + k], blocks)
            q = jnp.where(valid, cursor[b], spots - 1)
            cursor[b] = q + 1
            request = jnp.maximum(code - 1, 0)
            in_list = request // QB
            out[q] = jnp.where(valid, fixed + in_list * 65537, 0)
            out[spots + q] = jnp.where(valid, request % QB + 65536, 0)
        return carry

    lax.fori_loop(0, devices, settle, 0)


def spread(packed, out, group):
    lane_group = lax.broadcasted_iota(I32, (1, BLK), 1) // group
    for i in range(SUB):
        part = jnp.where(lane_group == i, packed, jnp.zeros_like(packed))
        part = part + pltpu.roll(part, 2 * group, axis=1)
        out[pl.ds(i, packed.shape[0], stride=SUB), :] = part + pltpu.roll(part, group, axis=1)


def score_kernel(n_pieces, group, sizes, plan_ref, *refs):
    plan = Plan(plan_ref, *sizes)
    pieces = refs[:n_pieces]
    vectors, logs, positions, exp_out, loc_out, totals_out, pos_out = refs[n_pieces : n_pieces + 7]
    users, p_rep, t_acc, p_acc, sems = refs[n_pieces + 7 :]
    copies = piece_copies(pieces, users, sems, 0, NQ * group, NQ * group + HEAD)
    for copy in copies:
        copy.start()
    t_acc[...] = jnp.zeros_like(t_acc)
    p_acc[...] = jnp.zeros_like(p_acc)
    spread(positions[...], p_rep, group)
    rows_iota = lax.broadcasted_iota(I32, (BLK, BLK), 0)
    lane_group = lax.broadcasted_iota(I32, (1, BLK), 1) // group
    for copy in copies:
        copy.wait()

    def chunk(c):
        first = pl.multiple_of(plan.cblk(c) * BLK, BLK)
        block = vectors[pl.ds(first, BLK), :]
        members = jnp.concatenate(
            [users[pl.ds(pl.multiple_of(plan.ul(c * SUB + i) * group, group), group), :] for i in range(SUB)],
            axis=0,
        )
        dots = lax.dot_general(block, members, (((1,), (1,)), ((), ())), preferred_element_type=F32)
        scores = LOGIT_SCALE * dots - logs[pl.ds(first, BLK), :]
        exp_scores = jnp.exp(scores)
        exp_out[pl.ds(pl.multiple_of(c * BLK, BLK), BLK), :] = exp_scores
        loc = jnp.full((1, BLK), -1, I32)
        masks = []
        for i in range(SUB):
            spot = c * SUB + i
            mask = jnp.logical_and(lane_group == i, plan.vq(spot) > 0)
            masks.append(mask)
            loc = jnp.where(mask, p_rep[pl.ds(plan.ul(spot), 1), :] - plan.kq(spot) * BLK, loc)
        loc_out[pl.ds(c, 1), :] = loc
        chosen = jnp.where(rows_iota == loc, scores, 0.0)
        return masks, jnp.sum(exp_scores, axis=0, keepdims=True), jnp.sum(chosen, axis=0, keepdims=True)

    def step(q, carry):
        done = [chunk(q * UNROLL + j) for j in range(UNROLL)]
        for j, (masks, total, chosen) in enumerate(done):
            for i in range(SUB):
                row = plan.tl((q * UNROLL + j) * SUB + i)
                t_acc[pl.ds(row, 1), :] += jnp.where(masks[i], total, 0.0)
                p_acc[pl.ds(row, 1), :] += jnp.where(masks[i], chosen, 0.0)
        return carry

    lax.fori_loop(0, (plan.nch() + UNROLL - 1) // UNROLL, step, 0)
    packed_rows = totals_out.shape[0]
    for acc, out in ((t_acc, totals_out), (p_acc, pos_out)):
        value = acc[...]
        both = value + pltpu.roll(value, 2 * group, axis=1)
        acc[...] = both + pltpu.roll(both, group, axis=1)
        packed = jnp.zeros((packed_rows, BLK), F32)
        for i in range(SUB):
            packed += jnp.where(lane_group == i, acc[pl.ds(i, packed_rows, stride=SUB), :], 0.0)
        out[...] = packed


def vector_kernel(group, scale, columns, sizes, plan_ref, *refs):
    plan = Plan(plan_ref, *sizes)
    vectors, exp_in, loc, totals, keep_out, send_out, grad_out, t_rep, v_acc, sem = refs
    v_acc[...] = jnp.zeros_like(v_acc)
    rows_iota = lax.broadcasted_iota(I32, (BLK, BLK), 0)
    lane_group = lax.broadcasted_iota(I32, (1, BLK), 1) // group
    spread(scale / totals[...], t_rep, group)
    low, high = columns

    def chunk(c):
        first = pl.multiple_of(plan.cblk(c) * BLK, BLK)
        weight = jnp.zeros((1, BLK), F32)
        for i in range(SUB):
            keep = jnp.logical_and(lane_group == i, plan.vq(c * SUB + i) > 0)
            weight += jnp.where(keep, t_rep[pl.ds(plan.tl(c * SUB + i), 1), :], 0.0)
        is_positive = rows_iota == loc[pl.ds(c, 1), :]
        here = pl.multiple_of(c * BLK, BLK)
        grad = (exp_in[pl.ds(here, BLK), :] * weight - jnp.where(is_positive, scale, 0.0)).astype(BF16)
        grad_out[pl.ds(here, BLK), :] = grad
        block = vectors[pl.ds(first, BLK), low:high]
        return lax.dot_general(grad, block, (((0,), (0,)), ((), ())), preferred_element_type=F32)

    def step(q, carry):
        parts = [chunk(q * UNROLL + j) for j in range(UNROLL)]
        for j in range(UNROLL):
            for i in range(SUB):
                start = pl.multiple_of(plan.ul((q * UNROLL + j) * SUB + i) * group, group)
                v_acc[pl.ds(start, group), :] += parts[j][i * group : (i + 1) * group]
        return carry

    lax.fori_loop(0, (plan.nch() + UNROLL - 1) // UNROLL, step, 0)
    half = v_acc.shape[0] // 2
    copy = pltpu.make_async_copy(v_acc.at[pl.ds(0, half), :], keep_out, sem)
    copy.start()
    send_out[...] = (LOGIT_SCALE * v_acc[pl.ds(half, half), :]).astype(BF16)
    copy.wait()


def item_kernel(n_pieces, group, tile_blocks, sizes, plan_ref, *refs):
    plan = Plan(plan_ref, *sizes)
    pieces = refs[:n_pieces]
    tower, grads, out_gradient, users, items, sems = refs[n_pieces:]
    tile = pl.program_id(0)

    @pl.when(tile == 0)
    def _():
        copies = piece_copies(pieces, users, sems, 0, NQ * group, NQ * group + HEAD)
        for copy in copies:
            copy.start()
        for copy in copies:
            copy.wait()

    items[...] = jnp.zeros_like(items)
    end = plan.starts(tile + 1)

    def chunk(c):
        members = jnp.concatenate(
            [users[pl.ds(pl.multiple_of(plan.ul(c * SUB + i) * group, group), group), :] for i in range(SUB)],
            axis=0,
        )
        grad = grads[pl.ds(pl.multiple_of(c * BLK, BLK), BLK), :]
        return jnp.dot(grad, members, preferred_element_type=F32)

    def step(q, carry):
        base = plan.starts(tile) + q * UNROLL
        parts = [chunk(base + j) for j in range(UNROLL)]
        for j in range(UNROLL):
            block = jnp.where(base + j < end, plan.cblk(base + j) - tile * tile_blocks, tile_blocks)
            first = pl.multiple_of(block * BLK, BLK)
            items[pl.ds(first, BLK), :] += parts[j]
        return carry

    lax.fori_loop(0, (end - plan.starts(tile) + UNROLL - 1) // UNROLL, step, 0)
    out = tower[...]
    gradient = LOGIT_SCALE * items[pl.ds(0, tile_blocks * BLK), :]
    norm = lax.rsqrt(jnp.sum(out * out, axis=1, keepdims=True) + NORM_EPSILON)
    projection = jnp.sum(out * gradient, axis=1, keepdims=True)
    out_gradient[...] = (gradient * norm - out * (projection * norm * norm * norm)).astype(BF16)


def weight_kernel(feats, hidden_t, second, out_gradient, first_out, second_out, first_t):
    tile = pl.program_id(0)

    @pl.when(tile == 0)
    def _():
        first_t[...] = jnp.zeros_like(first_t)
        second_out[...] = jnp.zeros_like(second_out)

    grad = out_gradient[...]
    hidden = hidden_t[...]
    second_out[...] += jnp.dot(hidden, grad, preferred_element_type=F32)
    act = lax.dot_general(second[...], grad, (((1,), (1,)), ((), ())), preferred_element_type=F32)
    act = jnp.where(hidden > 0, act, 0.0).astype(BF16)
    first_t[...] += jnp.dot(act, feats[...], preferred_element_type=F32)

    @pl.when(tile == pl.num_programs(0) - 1)
    def _():
        first_out[...] = first_t[...].T


def limit(mib):
    return pltpu.CompilerParams(vmem_limit_bytes=mib * 1024 * 1024)


def busy(micros):
    return pl.CostEstimate(flops=micros * 10**9, bytes_accessed=micros * 3 * 10**6, transcendentals=0)


def any_spec():
    return pl.BlockSpec(memory_space=pl.ANY)


def smem_spec():
    return pl.BlockSpec(memory_space=pltpu.SMEM)


def vmem_spec():
    return pl.BlockSpec(memory_space=pltpu.VMEM)


def body(
    item_feats, first_weight, second_weight, counts, user_embed, list_owner, list_slot, positive
):
    links = Links()
    devices = links.devices
    me = lax.axis_index(AXES)
    item_rows, _ = item_feats.shape
    own_blocks = item_rows // BLK
    user_rows, emb = user_embed.shape
    requests = list_slot.shape[0]
    capacity = 2 * requests // devices
    group = user_rows // NQ
    all_users = user_rows * devices
    slots = devices * capacity
    lists = devices * NQ
    core = 1 << links.core

    user_float = user_embed.astype(F32)
    user_norm = lax.rsqrt(jnp.sum(user_float * user_float, axis=1, keepdims=True) + NORM_EPSILON)
    user_vector = (user_float * user_norm).astype(BF16)

    masks, steps = gather_plan(links)
    order = [m for piece in masks for m in piece]
    order = order + [m ^ core for m in order]

    owners = list_owner[:, 0]
    same_owner = owners[:, None] == owners[None, :]
    request = jnp.arange(requests, dtype=I32)
    rank = jnp.sum((same_owner & (request[None, :] < request[:, None])).astype(I32), axis=1)
    position = owners * capacity + rank
    hit = position[:, None] == jnp.arange(slots, dtype=I32)[None, :]
    request_code = jnp.sum(jnp.where(hit, request[:, None] + 1, 0), axis=0)
    slot_code = jnp.sum(jnp.where(hit, list_slot[:, None], 0), axis=0)
    head = jnp.stack([request_code, slot_code, positive // BLK, positive % BLK])
    head = jnp.pad(head, ((0, HEAD - head.shape[0]), (0, 0))).astype(BF16)

    n_z = len(links.z)
    logs = jnp.log(counts.astype(F32)).astype(BF16).astype(F32)
    logs = jnp.broadcast_to(logs[:, None], (item_rows, BLK))
    first_t, second_t = first_weight.T, second_weight.T
    mask = steps[0][0]
    arrived, arrived_head = links.swap(user_vector, mask), links.swap(head, mask)
    arrived, logs, first_t, second_t = lax.optimization_barrier((arrived, logs, first_t, second_t))
    pieces = [join([user_vector, head]), join([arrived, arrived_head])]
    for index in range(1, n_z):
        mask, sources = steps[index]
        pieces.append(links.swap(join([pieces[s] for s in sources]), mask))
    for index in range(n_z, len(steps), 2):
        sent = [join([pieces[s] for s in sources]) for mask, sources in steps[index : index + 2]]
        if index + 2 >= len(steps):
            sent[0], sent[1], item_feats = lax.optimization_barrier((sent[0], sent[1], item_feats))
        sent = [links.swap(v, m) for v, (m, _) in zip(sent, steps[index : index + 2])]
        if index + 2 >= len(steps):
            hidden_t, tower_out, vectors = tower(item_feats, first_t, second_t)
            sent[0], sent[1], hidden_t, tower_out, vectors = lax.optimization_barrier(
                (sent[0], sent[1], hidden_t, tower_out, vectors)
            )
        pieces += sent
    other = [links.swap(piece, core) for piece in pieces]
    all_pieces = pieces + other

    max_chunks = (slots + (SUB - 1) * own_blocks) // SUB + UNROLL + 1
    max_chunks += -max_chunks % 8
    spots = max_chunks * SUB
    tile_blocks = TILE // BLK
    n_tiles = item_rows // TILE
    column = me * capacity
    n_pieces = len(all_pieces)
    packed_rows = all_users // BLK
    i32 = functools.partial(jax.ShapeDtypeStruct, dtype=I32)
    sizes = (spots, n_tiles)
    plan, positions = pl.pallas_call(
        functools.partial(plan_kernel, n_pieces, capacity, tile_blocks, sizes),
        out_shape=(i32((Plan(None, *sizes).size,)), i32((packed_rows, BLK))),
        in_specs=[smem_spec()] * 2 + [any_spec()] * n_pieces,
        out_specs=(smem_spec(), vmem_spec()),
        scratch_shapes=[
            pltpu.VMEM((devices * HEAD, emb), BF16),
            pltpu.VMEM((devices * HEAD, BLK), F32),
            pltpu.VMEM((devices * HEAD, BLK), F32),
            pltpu.VMEM((2 * devices, BLK), I32),
            pltpu.SMEM((2 * devices, BLK), I32),
            pltpu.SMEM((own_blocks + 1,), I32),
            pltpu.SMEM((own_blocks + 1,), I32),
            pltpu.SemaphoreType.DMA((devices,)),
        ],
        name="plan",
        cost_estimate=busy(6),
    )(jnp.stack([column % BLK, me, column // BLK]), jnp.asarray(np.array(order), I32), *all_pieces)
    exp_scores, local, totals, pos_part = pl.pallas_call(
        functools.partial(score_kernel, n_pieces, group, sizes),
        out_shape=(
            jax.ShapeDtypeStruct((max_chunks * BLK, BLK), F32),
            jax.ShapeDtypeStruct((max_chunks, BLK), I32),
            jax.ShapeDtypeStruct((packed_rows, BLK), F32),
            jax.ShapeDtypeStruct((packed_rows, BLK), F32),
        ),
        grid_spec=pltpu.PrefetchScalarGridSpec(
            num_scalar_prefetch=1,
            grid=(1,),
            in_specs=[any_spec()] * n_pieces + [vmem_spec()] * 3,
            out_specs=[vmem_spec()] * 4,
            scratch_shapes=[
                pltpu.VMEM((all_users, emb), BF16),
                pltpu.VMEM((lists, BLK), I32),
                pltpu.VMEM((lists, BLK), F32),
                pltpu.VMEM((lists, BLK), F32),
                pltpu.SemaphoreType.DMA((devices,)),
            ],
        ),
        compiler_params=limit(60),
        name="scores",
        cost_estimate=busy(9),
    )(plan, *all_pieces, vectors, logs, positions)

    for bit in [links.core] + links.x + links.y + links.z[::-1]:
        totals = totals + links.swap(totals, 1 << bit)

    width = emb if all_users <= 8192 else BLK
    half_users = all_users // 2
    keeps, sends = [], []
    for low in range(0, emb, width):
        kept, sent, score_grad = pl.pallas_call(
            functools.partial(vector_kernel, group, LOSS_SCALE / all_users, (low, low + width), sizes),
            out_shape=(
                jax.ShapeDtypeStruct((half_users, width), F32),
                jax.ShapeDtypeStruct((half_users, width), BF16),
                jax.ShapeDtypeStruct((max_chunks * BLK, BLK), BF16),
            ),
            grid_spec=pltpu.PrefetchScalarGridSpec(
                num_scalar_prefetch=1,
                grid=(1,),
                in_specs=[vmem_spec()] * 4,
                out_specs=[any_spec(), vmem_spec(), vmem_spec()],
                scratch_shapes=[
                    pltpu.VMEM((lists, BLK), F32),
                    pltpu.VMEM((all_users, width), F32),
                    pltpu.SemaphoreType.DMA,
                ],
            ),
            compiler_params=limit(60),
            name="vector_grads",
            cost_estimate=busy(12),
        )(plan, vectors, exp_scores, local, totals)
        keeps.append(kept)
        sends.append(sent)
    keep = keeps[0] if len(keeps) == 1 else jnp.concatenate(keeps, axis=1)
    send = sends[0] if len(sends) == 1 else jnp.concatenate(sends, axis=1)

    out_gradient = pl.pallas_call(
        functools.partial(item_kernel, n_pieces, group, tile_blocks, sizes),
        out_shape=jax.ShapeDtypeStruct((item_rows, emb), BF16),
        grid_spec=pltpu.PrefetchScalarGridSpec(
            num_scalar_prefetch=1,
            grid=(n_tiles,),
            in_specs=[any_spec()] * n_pieces
            + [pl.BlockSpec((TILE, emb), lambda t, *_: (t, 0)), vmem_spec()],
            out_specs=pl.BlockSpec((TILE, emb), lambda t, *_: (t, 0)),
            scratch_shapes=[
                pltpu.VMEM((all_users, emb), BF16),
                pltpu.VMEM((TILE + BLK, emb), F32),
                pltpu.SemaphoreType.DMA((devices,)),
            ],
        ),
        compiler_params=limit(60),
        name="item_grads",
        cost_estimate=busy(10),
    )(plan, *all_pieces, tower_out, score_grad)

    small_bits = [links.core] + links.x + links.y + links.z[::-1]
    small = iter(small_bits)

    def pos_stage(pos):
        bit = next(small, None)
        return pos if bit is None else pos + links.swap(pos, 1 << bit)

    arrived = links.swap(send, core)
    pos_part = pos_stage(pos_part)
    arrived, pos_part, out_gradient = lax.optimization_barrier((arrived, pos_part, out_gradient))
    partial, offset = [], 0
    for piece in masks:
        rows = slice(offset, offset + len(piece) * user_rows)
        partial.append(LOGIT_SCALE * keep[rows] + arrived[rows].astype(F32))
        offset = rows.stop
    outgoing = [partial[-1].astype(BF16), partial[-2].astype(BF16)]
    outgoing[0], outgoing[1], out_gradient = lax.optimization_barrier(
        (outgoing[0], outgoing[1], out_gradient)
    )

    def receive(partial, index, outgoing=None):
        if outgoing is None:
            outgoing = partial[index + 1].astype(BF16)
        return links.swap(outgoing, steps[index][0])

    def back(partial, index, arrived):
        offset = 0
        partial = list(partial)
        for s in steps[index][1]:
            rows = partial[s].shape[0]
            partial[s] = partial[s] + arrived[offset : offset + rows].astype(F32)
            offset += rows
        return partial

    feat, hid = first_weight.shape
    first_gradient, second_gradient = pl.pallas_call(
        weight_kernel,
        out_shape=(
            jax.ShapeDtypeStruct((feat, hid), F32),
            jax.ShapeDtypeStruct((hid, emb), F32),
        ),
        grid=(n_tiles,),
        in_specs=[
            pl.BlockSpec((TILE, feat), lambda t: (t, 0)),
            pl.BlockSpec((hid, TILE), lambda t: (0, t)),
            vmem_spec(),
            pl.BlockSpec((TILE, emb), lambda t: (t, 0)),
        ],
        out_specs=[vmem_spec(), vmem_spec()],
        scratch_shapes=[pltpu.VMEM((hid, feat), F32)],
        compiler_params=limit(60),
        name="weight_grads",
        cost_estimate=busy(13),
    )(item_feats, hidden_t, second_weight, out_gradient)
    fold = hid // emb
    tall = hid // fold
    packed = jnp.concatenate(
        [first_gradient]
        + [jnp.concatenate([second_gradient[i * tall : (i + 1) * tall] for i in range(fold)], axis=1)],
        axis=0,
    )
    index = len(steps) - 1
    arrived = [receive(partial, index, outgoing[0]), receive(partial, index - 1, outgoing[1])]
    arrived[0], arrived[1], packed = lax.optimization_barrier((arrived[0], arrived[1], packed))
    partial = back(back(partial, index, arrived[0]), index - 1, arrived[1])
    index -= 2
    weights = WeightSum(links, me, packed)
    state = weights.core_stage()
    pos_part = pos_stage(pos_part)
    while index > n_z:
        if index == n_z + 1:
            state = weights.plane_stage(state)
        arrived = [receive(partial, index), receive(partial, index - 1)]
        pos_part = pos_stage(pos_part)
        arrived[0], arrived[1], pos_part, state = lax.optimization_barrier(
            (arrived[0], arrived[1], pos_part, state)
        )
        partial = back(back(partial, index, arrived[0]), index - 1, arrived[1])
        index -= 2
    for stage in (weights.line_sum, weights.line_spread):
        state = stage(state)
        arrived = receive(partial, index)
        pos_part = pos_stage(pos_part)
        arrived, pos_part, state = lax.optimization_barrier((arrived, pos_part, state))
        partial = back(partial, index, arrived)
        index -= 1
    total = weights.spread_stage(state)
    for bit in small:
        pos_part = pos_part + links.swap(pos_part, 1 << bit)

    own_rows = user_rows // BLK
    own_totals = lax.dynamic_slice(totals, (me * own_rows, 0), (own_rows, BLK))
    own_pos = lax.dynamic_slice(pos_part, (me * own_rows, 0), (own_rows, BLK))
    user_loss = (jnp.log(own_totals) - own_pos).reshape(user_rows)
    vector_grad = partial[0]
    user_projection = jnp.sum(user_float * vector_grad, axis=1, keepdims=True)
    user_gradient = vector_grad * user_norm - user_float * (
        user_projection * user_norm * user_norm * user_norm
    )
    first_total = total[:feat].astype(F32)
    second_total = jnp.concatenate(
        [total[feat:, i * emb : (i + 1) * emb] for i in range(fold)], axis=0
    ).astype(F32)
    return (user_loss, user_gradient, first_total, second_total)


def tower(item_feats, first_t, second_t):
    rows, feat = item_feats.shape
    emb, hid = second_t.shape
    return pl.pallas_call(
        tower_kernel,
        out_shape=(
            jax.ShapeDtypeStruct((hid, rows), BF16),
            jax.ShapeDtypeStruct((rows, emb), F32),
            jax.ShapeDtypeStruct((rows, emb), BF16),
        ),
        grid=(rows // TILE,),
        in_specs=[
            pl.BlockSpec((TILE, feat), lambda t: (t, 0)),
            vmem_spec(),
            vmem_spec(),
        ],
        out_specs=[
            pl.BlockSpec((hid, TILE), lambda t: (0, t)),
            pl.BlockSpec((TILE, emb), lambda t: (t, 0)),
            pl.BlockSpec((TILE, emb), lambda t: (t, 0)),
        ],
        compiler_params=limit(60),
        name="tower",
        cost_estimate=busy(11),
    )(item_feats, first_t, second_t)


class WeightSum:
    def __init__(self, links, me, value):
        self.links = links
        self.value = value
        self.half = value.shape[0] // 2
        self.core_bit = (me >> links.core) & 1
        self.plane = links.x + links.y
        self.ways = 1 << len(self.plane)
        self.part = self.half // self.ways
        self.place = (me >> links.z[1]) & 3
        self.own = sum(((me >> bit) & 1) << i for i, bit in enumerate(self.plane))

    def mask_of(self, way):
        return sum(1 << bit for i, bit in enumerate(self.plane) if (way >> i) & 1)

    def core_stage(self):
        half = self.half
        send = lax.dynamic_slice_in_dim(self.value, (1 - self.core_bit) * half, half, 0)
        mine = lax.dynamic_slice_in_dim(self.value, self.core_bit * half, half, 0)
        return mine + self.links.swap(send, 1 << self.links.core)

    def plane_stage(self, mine):
        arrived = []
        for way in range(1, self.ways):
            out = lax.dynamic_slice_in_dim(mine, (self.own ^ way) * self.part, self.part, 0)
            arrived.append(self.links.swap(out.astype(BF16), self.mask_of(way)))
        own_sum = lax.dynamic_slice_in_dim(mine, self.own * self.part, self.part, 0)
        for item in arrived:
            own_sum = own_sum + item.astype(F32)
        return own_sum

    def line_masks(self):
        low, high = self.links.z[1], self.links.z[0]
        return [1 << low, 1 << high, (1 << low) | (1 << high)]

    def line_sum(self, own_sum):
        rows = own_sum.shape[0] // 4
        arrived = []
        for way, mask in enumerate(self.line_masks(), 1):
            out = lax.dynamic_slice_in_dim(own_sum, (self.place ^ way) * rows, rows, 0)
            arrived.append(self.links.swap(out.astype(BF16), mask))
        total = lax.dynamic_slice_in_dim(own_sum, self.place * rows, rows, 0)
        for item in arrived:
            total = total + item.astype(F32)
        return total.astype(BF16)

    def line_spread(self, final):
        parts = [final] + [self.links.swap(final, mask) for mask in self.line_masks()]
        return self.arrange(parts, self.place)

    def arrange(self, parts, own):
        ways = len(parts)
        for i in range(ways.bit_length() - 1):
            bit = (own >> i) & 1
            step = 1 << i
            parts = [jnp.where(bit == 1, parts[q ^ step], parts[q]) for q in range(ways)]
        return jnp.concatenate(parts, axis=0)

    def spread_stage(self, final):
        ways = self.ways
        parts = [final] + [self.links.swap(final, self.mask_of(way)) for way in range(1, ways)]
        near = self.arrange(parts, self.own)
        far = self.links.swap(near, 1 << self.links.core)
        first = self.core_bit == 0
        return jnp.concatenate([jnp.where(first, near, far), jnp.where(first, far, near)], axis=0)


def solution(mesh):
    return jax.shard_map(
        body,
        mesh=mesh,
        in_specs=(
            P(("user", "item"), None),
            P(),
            P(),
            P(("user", "item")),
            P(("user", "item"), None),
            P(("user", "item"), None),
            P(("user", "item")),
            P(("user", "item")),
        ),
        out_specs=(P(("user", "item")), P(("user", "item"), None), P(), P()),
        check_vma=False,
    )
```
